32 devices in a mesh: head: 8 (over y, x, core), seq: 4 (over z).
Axes of the slice: x: 2, y: 2, z: 4, core: 2. Of those that a mesh axis runs over, the one named last changes fastest.
Arguments:
- hidden_in: bfloat16 [2, 2048, 2048], P(None, ('head', 'seq')), may hold values from -6 to 6
- doc_lengths: int32 [2, 8], replicated, may hold values from 1 to 1024, 2048 in all within a row
- expert_ids: int32 [2, 2048, 8], P(None, ('head', 'seq')), may hold values from 0 to 15, all different within a row; in each aligned block of 64 rows (0 to 63, 64 to 127, ..., all dimensions but the last counted through in order) at most 48 rows name the same one
- out_grad: bfloat16 [2, 2048, 2048], P(None, ('head', 'seq')), may hold values from -6 to 6
- norm1_gain: bfloat16 [2048], replicated, may hold values from 0.099609375 to 1.8984375
- w_query: bfloat16 [2048, 2048], P(('head', 'seq')), may hold values from -0.125 to 0.125
- w_key: bfloat16 [2048, 2048], P(('head', 'seq')), may hold values from -0.125 to 0.125
- w_value: bfloat16 [2048, 2048], P(('head', 'seq')), may hold values from -0.125 to 0.125
- query_gain: bfloat16 [2048], replicated, may hold values from 0.099609375 to 1.8984375
- key_gain: bfloat16 [2048], replicated, may hold values from 0.099609375 to 1.8984375
- w_out: bfloat16 [2048, 2048], P(('head', 'seq')), may hold values from -2 to 2
- norm2_gain: bfloat16 [2048], replicated, may hold values from 0.099609375 to 1.8984375
- w_router: bfloat16 [2048, 16], replicated, may hold values from -0.0625 to 0.0625
- w_gate: bfloat16 [2048, 16, 1024], P('seq', 'head'), may hold values from -0.125 to 0.125
- w_up: bfloat16 [2048, 16, 1024], P('seq', 'head'), may hold values from -0.125 to 0.125
- w_down: bfloat16 [2048, 16, 1024], P('seq', 'head'), may hold values from -2 to 2
Outputs:
- hidden_out: bfloat16 [2, 2048, 2048], P(None, ('head', 'seq'))
- hidden_grad: bfloat16 [2, 2048, 2048], P(None, ('head', 'seq'))
- grad_norm1_gain: float32 [2048], P(('head', 'seq'))
- grad_w_query: float32 [2048, 2048], P(('head', 'seq'))
- grad_w_key: float32 [2048, 2048], P(('head', 'seq'))
- grad_w_value: float32 [2048, 2048], P(('head', 'seq'))
- grad_query_gain: float32 [2048], P(('head', 'seq'))
- grad_key_gain: float32 [2048], P(('head', 'seq'))
- grad_w_out: float32 [2048, 2048], P(('head', 'seq'))
- grad_norm2_gain: float32 [2048], P(('head', 'seq'))
- grad_w_router: float32 [2048, 16], P(('head', 'seq'))
- grad_w_gate: float32 [2048, 16, 1024], P('seq', 'head')
- grad_w_up: float32 [2048, 16, 1024], P('seq', 'head')
- grad_w_down: float32 [2048, 16, 1024], P('seq', 'head')
The draws below stay inside these ranges and needn't reach their ends.
Inputs may be any that keep to these rules, and one draw needn't show every extreme that they name: `doc_lengths`: in each micro-batch the 8 document lengths sum to 2048, and the longest is exactly 1024. `expert_ids`: each token names 8 different experts. In each aligned block of 64 tokens of one micro-batch (here half of one device's 128 tokens there) no expert is named more than 48 times, and in some blocks one is named exactly 48 times.
All inputs are finite; a program needn't handle non-finite values.
Results may differ from the reference program's by a relative error of at most 0.025.
Values may be sent and summed in bfloat16 or wider, within the bound.
No kernel may reach another device: no remote copies, remote signals or barrier semaphores. Data moves between devices by JAX's collectives and lax.ppermute only.
A program may use at most 320 MiB of HBM per device.

```python
import math
import jax
import jax.numpy as jnp
import numpy as np
from jax import lax

D = 2048
H = 16
HD = 128
F = 1024
TOPK = 8
CH = 64
MB = 2
NDOC = 8
E = 16
S = 2048
DOCMAX = 1024
CAP = 48


def level_of(key, dims, pieces, smallest, largest):
    factor_of = 1.0
    for axis_at, shards_of in pieces:
        draws = jax.random.uniform(jax.random.fold_in(jax.random.fold_in(key, 6), axis_at), (shards_of,), jnp.float32, smallest / len(pieces), largest / len(pieces))
        factor_of = factor_of * jnp.repeat(jnp.exp(draws), dims[axis_at] // shards_of).reshape((-1,) + (1,) * (len(dims) - 1 - axis_at))
    return factor_of


def length_profile(count, total, most, slope):
    loads = [(1 << 20) // math.isqrt(rank ** slope) + 1 for rank in range(2, count + 1)]
    surplus, counts = total - most - (count - 1), [1] * (count - 1)
    while surplus > 0:
        movable = [i for i in range(count - 1) if counts[i] < most]
        whole, left = sum([loads[i] for i in movable]), surplus
        for i in movable:
            addition = min(most - counts[i], max(1, left * loads[i] // whole), surplus)
            counts[i] = counts[i] + addition
            surplus = surplus - addition
    return np.array([most] + counts)


def ragged(stream_key, number_of, total, reach, lean):
    if number_of == 2:
        one = jax.random.randint(stream_key, (), max(1, total - reach), min(reach, total - 1) + 1)
        return jnp.stack([one, total - one])
    tallies = jnp.asarray(length_profile(number_of, total, reach, lean), jnp.int32)
    couples = (number_of - 1) // 2
    donor, receiver = tallies[1:1 + 2 * couples:2], tallies[2:2 + 2 * couples:2]
    margin = jnp.minimum(donor - 1, reach - receiver)
    moved = jax.random.randint(jax.random.fold_in(stream_key, 1), (couples,), 0, 1 << 20) % (margin + 1)
    tallies = tallies.at[1:1 + 2 * couples:2].set(donor - moved).at[2:2 + 2 * couples:2].set(receiver + moved)
    return tallies[jax.random.permutation(jax.random.fold_in(stream_key, 2), number_of)]


def routed_block(rng, own, number, rows, number_of, top, most, slope):
    ranking = jax.random.permutation(rng, number_of)
    crowded, ordinary = load_shares(number_of, rows * top, most, slope, True), load_shares(number_of, rows * top, most, slope, False)
    places = jnp.arange(number_of)

    def named(sizes, rotation):
        used = int((sizes > 0).sum())
        fixed = max(1, used // 4)
        shifted = fixed + (places - fixed + rotation * (used - fixed)) % max(1, number_of - fixed)
        return jnp.zeros((number_of,), jnp.int32).at[ranking[jnp.where(places < fixed, places, shifted)]].set(jnp.asarray(sizes, jnp.int32))

    sizes = jnp.where(number % 4 == 0, named(crowded, number // 4), named(ordinary, number - number // 4 - 1))
    mixed = jax.random.permutation(jax.random.fold_in(own, 3), number_of)
    donor, taker = mixed[0:number_of // 2 * 2:2], mixed[1:number_of // 2 * 2:2]
    room = jnp.minimum(sizes[donor] - 1, most - sizes[taker]) // 2
    room = jnp.where((donor == ranking[0]) | (taker == ranking[0]) | (sizes[taker] == 0), 0, jnp.maximum(room, 0))
    shifted = jax.random.randint(jax.random.fold_in(own, 4), (number_of // 2,), 0, 1 << 20) % (room + 1)
    sizes = sizes.at[donor].add(-shifted).at[taker].add(shifted)
    labels = jnp.searchsorted(jnp.cumsum(sizes), jnp.arange(rows * top), side="right").astype(jnp.int32)
    table = labels.reshape(top, rows).T
    table = table[jax.random.permutation(jax.random.fold_in(own, 1), rows)]
    rotation = jax.random.randint(jax.random.fold_in(own, 2), (rows, 1), 0, top)
    return jnp.take_along_axis(table, (jnp.arange(top)[None, :] + rotation) % top, axis=1)


def load_shares(amount, total, limit, skew, full):
    weights = [(1 << 20) // math.isqrt(rank ** skew) + 1 for rank in range(1, amount + 1)]
    largest = limit if full else min(limit, max(-(-total // amount), total * weights[0] // sum(weights)))
    least = 1 if total - largest >= amount - 1 else 0
    counts, spare = [largest] + [least] * (amount - 1), total - largest - least * (amount - 1)
    while spare > 0:
        free = [i for i in range(1, amount) if counts[i] < largest] or [i for i in range(1, amount) if counts[i] < limit]
        whole, left = sum([weights[i] for i in free]), spare
        for i in free:
            addition = min(limit - counts[i], max(1, left * weights[i] // whole), spare)
            counts[i] = counts[i] + addition
            spare = spare - addition
    return np.array(counts)


def scatter_about(stream_key, dims, spread, most, shards=(), kind=jnp.bfloat16):
    array = spread * jax.random.normal(stream_key, dims, jnp.float32)
    if shards:
        array = array * level_of(stream_key, dims, shards, -0.22, 0.18)
    return jnp.clip(array, -most, most).astype(kind)


def setup_inputs(seed: int = 0) -> dict:
    splits = jax.random.split(jax.random.key(seed), 17)
    hidden_in = scatter_about(splits[0], (MB, S, D), 1.0, 6.0, ((1, 32),))
    doc_lengths = jax.vmap(lambda own: ragged(own, NDOC, S, DOCMAX, 2))(jax.random.split(splits[1], MB)).reshape((MB, NDOC)).astype(jnp.int32)
    expert_ids_keys = jax.random.split(jax.random.fold_in(splits[2], 1), MB * S // CH)
    expert_ids_turns = jax.random.permutation(jax.random.fold_in(splits[2], 3), MB * S // CH)
    expert_ids = jax.vmap(lambda own, number: routed_block(jax.random.fold_in(splits[2], 2), own, number, CH, E, TOPK, CAP, 1))(expert_ids_keys, expert_ids_turns).reshape((MB, S, TOPK))
    out_grad = scatter_about(splits[3], (MB, S, D), 1.0, 6.0, ((1, 32),))
    norm1_gain = jnp.clip(1.0 + 0.18 * jax.random.normal(splits[4], (D,), jnp.float32), 0.099609375, 1.8984375).astype(jnp.bfloat16)
    w_query = scatter_about(splits[5], (D, H * HD), D ** -0.5, 0.125, ((0, 32),))
    w_key = scatter_about(splits[6], (D, H * HD), D ** -0.5, 0.125, ((0, 32),))
    w_value = scatter_about(splits[7], (D, H * HD), D ** -0.5, 0.125, ((0, 32),))
    query_gain = jnp.clip(1.0 + 0.18 * jax.random.normal(splits[8], (H * HD,), jnp.float32), 0.099609375, 1.8984375).astype(jnp.bfloat16)
    key_gain = jnp.clip(1.0 + 0.18 * jax.random.normal(splits[9], (H * HD,), jnp.float32), 0.099609375, 1.8984375).astype(jnp.bfloat16)
    w_out = scatter_about(splits[10], (H * HD, D), (H * HD // 256) ** -0.5, 2.0, ((0, 32),))
    norm2_gain = jnp.clip(1.0 + 0.18 * jax.random.normal(splits[11], (D,), jnp.float32), 0.099609375, 1.8984375).astype(jnp.bfloat16)
    w_router = scatter_about(splits[12], (D, E), (4 * D) ** -0.5, 0.0625)
    w_gate = scatter_about(splits[13], (D, E, F), D ** -0.5, 0.125, ((0, 4), (1, 8)))
    w_up = scatter_about(splits[14], (D, E, F), D ** -0.5, 0.125, ((0, 4), (1, 8)))
    w_down = scatter_about(splits[15], (D, E, F), (max(1, 2 * F // (E * E))) ** -0.5, 2.0, ((0, 4), (1, 8)))
    return dict(hidden_in=hidden_in, doc_lengths=doc_lengths, expert_ids=expert_ids, out_grad=out_grad, norm1_gain=norm1_gain, w_query=w_query, w_key=w_key, w_value=w_value, query_gain=query_gain, key_gain=key_gain, w_out=w_out, norm2_gain=norm2_gain, w_router=w_router, w_gate=w_gate, w_up=w_up, w_down=w_down)


eps = 1e-06
rope_base = 10000.0
exact_mode = lax.Precision.HIGHEST

@jax.custom_vjp
def low(v):
    return lax.optimization_barrier(v.astype(jnp.bfloat16)).astype(jnp.float32)

@jax.custom_vjp
def low_back(v):
    return v

def low_keep(v):
    return (low(v), None)

def low_pass(kept, grad):
    return (grad,)

def back_keep(v):
    return (v, None)

def back_low(kept, grad):
    return (low(grad),)
low.defvjp(low_keep, low_pass)
low_back.defvjp(back_keep, back_low)

def rms_scale(values):
    return lax.rsqrt(lax.optimization_barrier(jnp.mean(values * values, axis=-1, keepdims=True)) + eps)

def rotate(values, positions, direction):
    half_width = HD // 2
    frequency = rope_base ** (-jnp.arange(half_width, dtype=jnp.float32) * 2.0 / HD)
    angles = positions.astype(jnp.float32)[:, None] * frequency[None, :]
    cosine = jnp.cos(angles)[:, None, :]
    sine_table = direction * jnp.sin(angles)[:, None, :]
    first_half = values[..., :half_width]
    second = values[..., half_width:]
    return jnp.concatenate([first_half * cosine - second * sine_table, second * cosine + first_half * sine_table], axis=-1)

def segment_of(positions, lengths):
    starts = jnp.cumsum(lengths) - lengths
    return lax.optimization_barrier(jnp.sum((positions[:, None] >= starts[None, :]).astype(jnp.int32), axis=1)) - 1

def attention(queries, key_rows, value_rows, segments):
    seq_len = queries.shape[0]
    block_rows = min(512, seq_len)
    block_count = seq_len // block_rows

    def one_block(block_args):
        query_block, seg_block = block_args
        scores = jnp.einsum('qhd,khd->hqk', query_block, key_rows, precision=exact_mode)
        scores = low_back(HD ** (-0.5) * scores)
        scores = jnp.where((seg_block[:, None] == segments[None, :])[None], scores, -1e+30)
        log_total = jax.nn.logsumexp(scores, axis=-1, keepdims=True)
        prob_rows = jnp.exp(scores - log_total)
        return jnp.einsum('hqk,khd->qhd', low(prob_rows), value_rows, precision=exact_mode)
    mixed_out = lax.map(jax.checkpoint(one_block), (queries.reshape(block_count, block_rows, H, HD), segments.reshape(block_count, block_rows)))
    return mixed_out.reshape(seq_len, H * HD)

def expert_mix(act_two, routes, router_probs, w_gate, w_up, w_down):
    chosen = (routes[:, :, None] == jnp.arange(E, dtype=jnp.int32)[None, None, :]).astype(router_probs.dtype)
    share_rows = lax.optimization_barrier(jnp.sum(chosen * router_probs[:, None, :], axis=1))

    def expert_step(running, packed):
        gate_weight, up_weight, down_weight, share_col = packed
        inputs = low_back(act_two)
        gate_pre = low_back(jnp.dot(inputs, gate_weight, precision=exact_mode))
        upward = low_back(jnp.dot(inputs, up_weight, precision=exact_mode))
        inner_act = low(jax.nn.silu(gate_pre) * upward)
        expert_out = low_back(low(jnp.dot(inner_act, down_weight.T, precision=exact_mode)))
        return (running + share_col[:, None] * expert_out, None)
    expert_sum, unused = lax.scan(jax.checkpoint(expert_step), jnp.zeros(act_two.shape, act_two.dtype), (jnp.moveaxis(w_gate, 1, 0), jnp.moveaxis(w_up, 1, 0), jnp.moveaxis(w_down, 1, 0), share_rows.T))
    return expert_sum

def layer(hidden, weights, positions, segments, routes):
    norm1_gain, w_query, w_key, w_value, query_gain, key_gain, w_out, norm2_gain, w_router, w_gate, w_up, w_down = weights
    normed_one = hidden * rms_scale(hidden)
    act_one = low(normed_one * norm1_gain)
    query_pre = low_back(jnp.dot(act_one, w_query, precision=exact_mode))
    key_pre = low_back(jnp.dot(act_one, w_key, precision=exact_mode))
    value_rows = low_back(low(jnp.dot(act_one, w_value, precision=exact_mode)))
    query_rot = rotate((query_pre * rms_scale(query_pre) * query_gain).reshape(-1, H, HD), positions, 1.0)
    key_rot = rotate((key_pre * rms_scale(key_pre) * key_gain).reshape(-1, H, HD), positions, 1.0)
    queries = low_back(low(query_rot))
    key_rows = low_back(low(key_rot))
    mixed_out = attention(queries, key_rows, value_rows.reshape(-1, H, HD), segments)
    mixed_out = low_back(low(mixed_out))
    residual = hidden + low_back(jnp.dot(mixed_out, w_out, precision=exact_mode))
    act_two = low(residual * rms_scale(residual) * norm2_gain)
    logits = low_back(jnp.dot(act_two, w_router, precision=exact_mode))
    router_probs = jax.nn.softmax(logits, axis=-1)
    return residual + expert_mix(act_two, routes, router_probs, w_gate, w_up, w_down)

def reference(hidden_in, doc_lengths, expert_ids, out_grad, norm1_gain, w_query, w_key, w_value, query_gain, key_gain, w_out, norm2_gain, w_router, w_gate, w_up, w_down):
    params = tuple((weight.astype(jnp.float32) for weight in (norm1_gain, w_query, w_key, w_value, query_gain, key_gain, w_out, norm2_gain, w_router, w_gate, w_up, w_down)))
    positions = jnp.arange(S, dtype=jnp.int32)
    out_rows = []
    grad_rows = []
    grad_sums = None
    for micro_index in range(MB):
        segments = segment_of(positions, doc_lengths[micro_index])
        routes = expert_ids[micro_index]

        def apply_layer(hidden, weights):
            return layer(hidden, weights, positions, segments, routes)
        result, pullback = jax.vjp(apply_layer, hidden_in[micro_index].astype(jnp.float32), params)
        grad_hidden, grad_params = pullback(out_grad[micro_index].astype(jnp.float32))
        out_rows.append(result.astype(jnp.bfloat16))
        grad_rows.append(grad_hidden.astype(jnp.bfloat16))
        grad_sums = grad_params if grad_sums is None else tuple((earlier + later for earlier, later in zip(grad_sums, grad_params)))
    return (jnp.stack(out_rows), jnp.stack(grad_rows), grad_sums[0], grad_sums[1], grad_sums[2], grad_sums[3], grad_sums[4], grad_sums[5], grad_sums[6], grad_sums[7], grad_sums[8], grad_sums[9], grad_sums[10], grad_sums[11])
```

```python
import jax
import jax.numpy as jnp
from jax import lax
from jax.experimental import pallas as pl
from jax.experimental.pallas import tpu as pltpu
from jax.sharding import PartitionSpec as P

H = 16
HD = 128
TOPK = 8

eps = 1e-06
rope_base = 10000.0
bf16 = jnp.bfloat16
f32 = jnp.float32


def rms_scale(values):
    return lax.rsqrt(jnp.mean(values * values, axis=-1, keepdims=True) + eps)


def norm_back(grad_normed, normed, scale_rows):
    return scale_rows * (
        grad_normed - normed * jnp.mean(grad_normed * normed, axis=-1, keepdims=True)
    )


def swap(value, axis, bit):
    count = lax.axis_size(axis)
    return lax.ppermute(value, axis, [(i, i ^ (1 << bit)) for i in range(count)])


def bits_of(count):
    return count.bit_length() - 1


def spread(value, axis, order):
    bits = bits_of(lax.axis_size(axis))
    value = value.reshape((1,) * bits + value.shape)
    for bit in order:
        value = jnp.concatenate([value, swap(value, axis, bit)], axis=bits - 1 - bit)
    lead = 1
    for d in value.shape[:bits]:
        lead *= d
    return value.reshape((lead,) + value.shape[bits:])


def collect(value, axis, order, low=0):
    bits = bits_of(lax.axis_size(axis))
    rest = value.shape[1:]
    value = value.reshape((2,) * (bits - low) + (1,) * low + rest)
    for bit in order:
        at = bits - 1 - bit
        kept = lax.slice_in_dim(value, 0, 1, axis=at)
        sent = lax.slice_in_dim(value, 1, 2, axis=at)
        got = swap(sent, axis, bit)
        value = (kept.astype(f32) + got.astype(f32)).astype(value.dtype)
    return value.reshape(rest)


def total_over(value, axis, at):
    bits = bits_of(lax.axis_size(axis))
    shape = value.shape
    value = value.reshape(shape[:at] + (2,) * bits + shape[at + 1 :])
    for bit in range(bits):
        value = value + jnp.flip(swap(value, axis, bit), at + bits - 1 - bit)
    return value.reshape(shape)


def spread_halves(rows, axis, order):
    half = rows.shape[-2] // 2
    first = spread(rows[..., :half, :], axis, order)
    second = spread(rows[..., half:, :], axis, order[::-1])
    return jnp.concatenate([first, second], axis=-2)


def collect_halves(rows, axis, order, low):
    half = rows.shape[-2] // 2
    first = collect(rows[..., :half, :], axis, order[::-1], low)
    second = collect(rows[..., half:, :], axis, order, low)
    return jnp.concatenate([first, second], axis=-2)


def rotate(values, cosine, sine):
    half_width = HD // 2
    first_half = values[..., :half_width]
    second = values[..., half_width:]
    return jnp.concatenate(
        [first_half * cosine - second * sine, second * cosine + first_half * sine], axis=-1
    )


def segment_of(positions, lengths):
    count = lengths.shape[0]
    earlier = jnp.arange(count)[:, None] < jnp.arange(count)[None, :]
    starts = jnp.sum(jnp.where(earlier, lengths[:, None], 0), axis=0)
    return jnp.sum((positions[:, None] >= starts[None, :]).astype(jnp.int32), axis=1) - 1


score_scale = HD ** (-0.5)
by_rows = (((1,), (1,)), ((), ()))
by_first = (((0,), (0,)), ((), ()))


def attend_kernel(q_ref, k_ref, v_ref, sq_ref, sk_ref, o_ref, total_ref):
    scores = score_scale * lax.dot_general(
        q_ref[...], k_ref[...], by_rows, preferred_element_type=f32
    )
    scores = jnp.where(sq_ref[...] == sk_ref[...], scores, -1e30)
    most = jnp.max(scores, axis=1, keepdims=True)
    weights = jnp.exp(scores - most)
    total = jnp.sum(weights, axis=1, keepdims=True)
    mixed = jnp.dot(weights.astype(bf16), v_ref[...], preferred_element_type=f32)
    o_ref[...] = (mixed / total).astype(bf16)
    total_ref[...] = most + jnp.log(total)


def attend_back_kernel(
    q_ref, k_ref, v_ref, sq_ref, sk_ref, total_ref, g_ref, dq_ref, dk_ref, dv_ref, k_sum, v_sum
):
    step = pl.program_id(0)

    @pl.when(step == 0)
    def _():
        k_sum[...] = jnp.zeros_like(k_sum)
        v_sum[...] = jnp.zeros_like(v_sum)

    scores = score_scale * lax.dot_general(
        q_ref[...], k_ref[...], by_rows, preferred_element_type=f32
    )
    scores = jnp.where(sq_ref[...] == sk_ref[...], scores, -1e30)
    probs = jnp.exp(scores - total_ref[...])
    grad_probs = lax.dot_general(g_ref[...], v_ref[...], by_rows, preferred_element_type=f32)
    inner = jnp.sum(probs * grad_probs, axis=1, keepdims=True)
    grad_scores = (probs * (grad_probs - inner)).astype(bf16)
    dq_ref[...] = (
        score_scale * jnp.dot(grad_scores, k_ref[...], preferred_element_type=f32)
    ).astype(bf16)
    k_sum[...] += score_scale * lax.dot_general(
        grad_scores, q_ref[...], by_first, preferred_element_type=f32
    )
    v_sum[...] += lax.dot_general(
        probs.astype(bf16), g_ref[...], by_first, preferred_element_type=f32
    )

    @pl.when(step == pl.num_programs(0) - 1)
    def _():
        dk_ref[...] = k_sum[...].astype(bf16)
        dv_ref[...] = v_sum[...].astype(bf16)


def attend(queries, keys, values, seg_query, seg_key):
    rows, count = queries.shape[0], keys.shape[0]
    block = max(32, min(256, (1 << 19) // count, rows))
    by_block = lambda i: (i, 0)
    whole = lambda i: (0, 0)
    return pl.pallas_call(
        attend_kernel,
        grid=(rows // block,),
        in_specs=[
            pl.BlockSpec((block, HD), by_block),
            pl.BlockSpec((count, HD), whole),
            pl.BlockSpec((count, HD), whole),
            pl.BlockSpec((block, 1), by_block),
            pl.BlockSpec((1, count), whole),
        ],
        out_specs=[pl.BlockSpec((block, HD), by_block), pl.BlockSpec((block, 1), by_block)],
        out_shape=[
            jax.ShapeDtypeStruct((rows, HD), bf16),
            jax.ShapeDtypeStruct((rows, 1), f32),
        ],
        compiler_params=pltpu.CompilerParams(vmem_limit_bytes=40 << 20),
        name="attend",
    )(queries, keys, values, seg_query[:, None], seg_key[None, :])


def attend_back(queries, keys, values, seg_query, seg_key, totals, grad_mixed):
    rows, count = queries.shape[0], keys.shape[0]
    block = max(32, min(256, (1 << 19) // count, rows))
    by_block = lambda i: (i, 0)
    whole = lambda i: (0, 0)
    return pl.pallas_call(
        attend_back_kernel,
        grid=(rows // block,),
        in_specs=[
            pl.BlockSpec((block, HD), by_block),
            pl.BlockSpec((count, HD), whole),
            pl.BlockSpec((count, HD), whole),
            pl.BlockSpec((block, 1), by_block),
            pl.BlockSpec((1, count), whole),
            pl.BlockSpec((block, 1), by_block),
            pl.BlockSpec((block, HD), by_block),
        ],
        out_specs=[
            pl.BlockSpec((block, HD), by_block),
            pl.BlockSpec((count, HD), whole),
            pl.BlockSpec((count, HD), whole),
        ],
        out_shape=[
            jax.ShapeDtypeStruct((rows, HD), bf16),
            jax.ShapeDtypeStruct((count, HD), bf16),
            jax.ShapeDtypeStruct((count, HD), bf16),
        ],
        scratch_shapes=[pltpu.VMEM((count, HD), f32), pltpu.VMEM((count, HD), f32)],
        compiler_params=pltpu.CompilerParams(vmem_limit_bytes=48 << 20),
        name="attend_back",
    )(queries, keys, values, seg_query[:, None], seg_key[None, :], totals, grad_mixed)


def body(
    hidden_in,
    doc_lengths,
    expert_ids,
    out_grad,
    norm1_gain,
    w_query,
    w_key,
    w_value,
    query_gain,
    key_gain,
    w_out,
    norm2_gain,
    w_router,
    w_gate,
    w_up,
    w_down,
):
    heads_of = lax.axis_size("head")
    seqs = lax.axis_size("seq")
    head_index = lax.axis_index("head")
    seq_index = lax.axis_index("seq")
    micros, local, width = hidden_in.shape
    heads_here = H // heads_of
    cols = heads_here * HD
    experts_here = w_gate.shape[1]
    expert_count = experts_here * heads_of
    hidden_units = w_gate.shape[2]
    part_units = hidden_units // seqs
    tokens = micros * local
    stride = seqs * local
    slice_rows = heads_of * local
    head_bits = list(range(bits_of(heads_of)))
    chip_bits = head_bits[1:]
    seq_bits = list(range(bits_of(seqs)))
    row_iota = jnp.arange(local, dtype=jnp.int32)
    slots = jnp.arange(heads_of, dtype=jnp.int32)

    gain_one = norm1_gain.astype(f32)
    gain_two = norm2_gain.astype(f32)
    gain_query = lax.dynamic_slice(query_gain, (head_index * cols,), (cols,)).astype(f32)
    gain_key = lax.dynamic_slice(key_gain, (head_index * cols,), (cols,)).astype(f32)

    stacked = jnp.stack([w_query, w_key, w_value], axis=1)
    stacked = stacked.reshape(-1, 3, heads_of, cols).transpose(2, 0, 1, 3)
    weight_rows = stacked.shape[1]
    stacked = lax.all_to_all(
        stacked.reshape(heads_of, weight_rows, 3 * cols),
        "head",
        split_axis=0,
        concat_axis=0,
        tiled=True,
    )
    w_qkv = lax.all_gather(stacked, "seq", axis=1, tiled=True).reshape(width, 3 * cols)
    w_out_here = lax.all_gather(w_out, "seq", axis=0, tiled=True)

    def to_units(weight):
        rows = weight.shape[0]
        parts = weight.reshape(rows, experts_here, seqs, part_units).transpose(2, 0, 1, 3)
        parts = lax.all_to_all(
            parts.reshape(seqs, rows, experts_here * part_units),
            "seq",
            split_axis=0,
            concat_axis=0,
            tiled=True,
        )
        return parts.reshape(seqs * rows, experts_here * part_units)

    def both_cores(mine):
        return jnp.concatenate([mine, swap(mine, "head", 0)], axis=1)

    w_down_here = both_cores(to_units(w_down))
    w_gate_here = both_cores(to_units(w_gate))
    w_up_here = both_cores(to_units(w_up))
    w_gate_up = jnp.concatenate([w_gate_here, w_up_here], axis=1)
    unit_count = w_gate_here.shape[1]

    def gather_tokens(rows):
        rows = spread(rows, "seq", seq_bits[::-1])
        rows = spread_halves(rows, "head", chip_bits)
        return rows.reshape(-1, rows.shape[-1])

    def return_tokens(rows, length):
        rows = rows.reshape(heads_of // 2, seqs, length, rows.shape[-1])
        rows = collect_halves(rows, "head", chip_bits, 1)
        return collect(rows, "seq", seq_bits)

    grads_here = [gather_tokens(out_grad[m]) for m in range(micros)]

    def over_heads(sums):
        sums = total_over(sums.reshape(2, micros, heads_of, local), "head", 2)
        return sums.reshape(2, micros * slice_rows) / (heads_of * cols)

    hidden = hidden_in.reshape(tokens, width).astype(f32)
    scale_one = rms_scale(hidden)
    normed_one = hidden * scale_one
    act_one = (normed_one * gain_one).astype(bf16).reshape(micros, local, width)
    ag_order = chip_bits + [0]
    other_order = chip_bits[::-1] + [0]
    act_parts = [
        spread(act_one[m], "head", ag_order if m % 2 == 0 else other_order).reshape(
            slice_rows, width
        )
        for m in range(micros)
    ]
    act_slice = jnp.concatenate(act_parts, axis=0)
    qkv = jnp.dot(act_slice, w_qkv, preferred_element_type=f32)
    query_pre, key_pre, value_pre = qkv[:, :cols], qkv[:, cols : 2 * cols], qkv[:, 2 * cols :]
    squares = jnp.stack([jnp.sum(query_pre * query_pre, axis=1), jnp.sum(key_pre * key_pre, axis=1)])
    squares = over_heads(squares)
    query_scale = lax.rsqrt(squares[0] + eps)[:, None]
    key_scale = lax.rsqrt(squares[1] + eps)[:, None]
    query_normed = query_pre * query_scale
    key_normed = key_pre * key_scale

    slot_pos = ((head_index ^ slots) * stride + seq_index * local)[:, None] + row_iota[None, :]
    slot_pos = slot_pos.reshape(slice_rows)
    frequency = rope_base ** (-jnp.arange(HD // 2, dtype=f32) * 2.0 / HD)
    angles = slot_pos.astype(f32)[:, None] * frequency[None, :]
    cosine, sine = jnp.cos(angles), jnp.sin(angles)

    def turn(values, direction):
        shaped = values.reshape(micros, slice_rows, heads_here, HD)
        turned = rotate(shaped, cosine[None, :, None, :], direction * sine[None, :, None, :])
        return turned.reshape(values.shape)

    query_rot = turn(query_normed * gain_query, 1.0).astype(bf16)
    key_rot = turn(key_normed * gain_key, 1.0).astype(bf16)
    value_low = value_pre.astype(bf16)

    paired = heads_here * micros == seqs
    combos = heads_here * micros

    def to_pairs(values):
        kinds = values.shape[1] // cols
        values = values.reshape(micros, slice_rows, kinds, heads_here, HD)
        values = values.transpose(3, 0, 1, 2, 4).reshape(combos, slice_rows, kinds * HD)
        values = lax.all_to_all(values, "seq", split_axis=0, concat_axis=0, tiled=True)
        return values.reshape(seqs * slice_rows, kinds * HD)

    def from_pairs(values):
        kinds = values.shape[1] // HD
        values = lax.all_to_all(
            values.reshape(seqs, slice_rows, kinds * HD),
            "seq",
            split_axis=0,
            concat_axis=0,
            tiled=True,
        )
        values = values.reshape(heads_here, micros, slice_rows, kinds, HD)
        return values.transpose(1, 2, 3, 0, 4).reshape(micros * slice_rows, kinds * cols)

    all_pos = (
        ((head_index ^ slots) * stride)[None, :, None]
        + (jnp.arange(seqs, dtype=jnp.int32) * local)[:, None, None]
        + row_iota[None, None, :]
    ).reshape(seqs * slice_rows)
    if paired:
        triple = to_pairs(jnp.concatenate([query_rot, key_rot, value_low], axis=1))
        queries, keys, values = triple[:, :HD], triple[:, HD : 2 * HD], triple[:, 2 * HD :]
        segments = segment_of(all_pos, lax.dynamic_index_in_dim(doc_lengths, seq_index % micros, 0, False))
        mixed, totals = attend(queries, keys, values, segments, segments)
        mixed_slice = from_pairs(mixed)
    else:
        keys_all = lax.all_gather(key_rot.reshape(micros, slice_rows, cols), "seq", axis=1, tiled=True)
        values_all = lax.all_gather(value_low.reshape(micros, slice_rows, cols), "seq", axis=1, tiled=True)
        jobs = []
        pieces = []
        for m in range(micros):
            seg_key = segment_of(all_pos, doc_lengths[m])
            seg_query = segment_of(slot_pos, doc_lengths[m])
            row = []
            for a in range(heads_here):
                part = slice(a * HD, (a + 1) * HD)
                job = (
                    query_rot[m * slice_rows : (m + 1) * slice_rows, part],
                    keys_all[m][:, part],
                    values_all[m][:, part],
                    seg_query,
                    seg_key,
                )
                mixed, totals = attend(*job)
                jobs.append(job + (totals,))
                row.append(mixed)
            pieces.append(jnp.concatenate(row, axis=1))
        mixed_slice = jnp.concatenate(pieces, axis=0)

    def to_owner(partial):
        done = []
        for m in range(micros):
            part = partial[m * slice_rows : (m + 1) * slice_rows].reshape(heads_of, local, width)
            order = ag_order if m % 2 == 0 else other_order
            done.append(collect(part, "head", order[::-1]))
        return jnp.concatenate(done, axis=0).astype(f32)

    branch = to_owner(jnp.dot(mixed_slice, w_out_here, preferred_element_type=f32).astype(bf16))
    residual = hidden + branch
    scale_two = rms_scale(residual)
    normed_two = residual * scale_two
    act_two = (normed_two * gain_two).astype(bf16)
    logits = jnp.dot(act_two, w_router, preferred_element_type=f32)
    router_probs = jax.nn.softmax(logits, axis=-1)
    ids = expert_ids.reshape(tokens, TOPK)
    chosen = jnp.sum(
        (ids[:, :, None] == jnp.arange(expert_count, dtype=jnp.int32)[None, None, :]).astype(f32), axis=1
    )
    shares = (chosen * router_probs).reshape(micros, local, expert_count)

    def my_columns(table, index):
        return lax.dynamic_slice(table, (0, index * experts_here), (table.shape[0], experts_here))

    def widen(values):
        return jnp.repeat(values, part_units, axis=1)

    shares_all = spread(spread(jnp.swapaxes(shares, 0, 1), "seq", seq_bits[::-1]), "head", chip_bits)
    grad_acts, grad_routers, out_rows, states = [], [], [], []
    acts_here = []
    for m in range(micros):
        acts = gather_tokens(act_two.reshape(micros, local, width)[m])
        grads = grads_here[m]
        table = shares_all[:, :, :, m].reshape(-1, expert_count)
        gates = jnp.concatenate(
            [my_columns(table, head_index), my_columns(table, head_index ^ 1)], axis=1
        )
        gate_wide = widen(gates)
        gate_up = jnp.dot(acts, w_gate_up, preferred_element_type=f32)
        gate_pre, upward = gate_up[:, :unit_count], gate_up[:, unit_count:]
        grad_plain = jnp.dot(grads, w_down_here, preferred_element_type=f32)
        sigmoid_gate = jax.nn.sigmoid(gate_pre)
        inner = gate_pre * sigmoid_gate * upward
        inner_low = (inner * gate_wide).astype(bf16)
        grad_gate = jnp.sum((inner * grad_plain).reshape(-1, 2 * experts_here, part_units), axis=2)
        grad_inner = grad_plain * gate_wide
        grad_pre = (
            grad_inner * upward * sigmoid_gate * (1.0 + gate_pre * (1.0 - sigmoid_gate))
        ).astype(bf16)
        grad_up = (grad_inner * gate_pre * sigmoid_gate).astype(bf16)
        grad_both = jnp.concatenate([grad_pre, grad_up], axis=1)
        grad_part = lax.dot_general(grad_both, w_gate_up, by_rows, preferred_element_type=f32)
        grad_acts.append(return_tokens(grad_part.astype(bf16), local))
        lanes = jnp.arange(expert_count, dtype=jnp.int32)[None, :]
        placed = jnp.zeros((grad_gate.shape[0], expert_count), f32)
        for a in range(2 * experts_here):
            owner = (head_index ^ (a // experts_here)) * experts_here + a % experts_here
            placed = placed + jnp.where(lanes == owner, grad_gate[:, a : a + 1], 0.0)
        grad_routers.append(placed)
        out_part = lax.dot_general(inner_low, w_down_here, by_rows, preferred_element_type=f32)
        out_rows.append(return_tokens(out_part.astype(bf16), local))
        states.append((acts, grads, grad_both, inner_low))

    routers = jnp.stack(
        [r.reshape(heads_of // 2, seqs, local, expert_count) for r in grad_routers], axis=2
    )
    routers = collect(collect(routers, "head", chip_bits[::-1], 1), "seq", seq_bits)
    grad_router = routers.reshape(tokens, expert_count) * chosen
    expert_sum = jnp.concatenate(out_rows, axis=0).astype(f32)
    hidden_out = (residual + expert_sum).astype(bf16).reshape(micros, local, width)

    def weight_sum(pairs):
        total = None
        for left, right in pairs:
            part = lax.dot_general(left, right, by_first, preferred_element_type=f32)
            total = part if total is None else total + part
        return total

    def from_units(total):
        half = total.shape[1] // 2
        total = total[:, :half] + swap(total[:, half:].astype(bf16), "head", 0).astype(f32)
        parts = total.astype(bf16).reshape(seqs, width // seqs, experts_here * part_units)
        parts = lax.all_to_all(parts, "seq", split_axis=0, concat_axis=0, tiled=True)
        parts = parts.reshape(seqs, width // seqs, experts_here, part_units).transpose(1, 2, 0, 3)
        return parts.reshape(width // seqs, experts_here, hidden_units).astype(f32)

    grad_w_down = from_units(weight_sum([(s[1], s[3]) for s in states]))
    grad_gate_up = weight_sum([(s[0], s[2]) for s in states])
    grad_w_gate = from_units(grad_gate_up[:, :unit_count])
    grad_w_up = from_units(grad_gate_up[:, unit_count:])

    grad_logits = (
        router_probs * (grad_router - jnp.sum(router_probs * grad_router, axis=-1, keepdims=True))
    ).astype(bf16)
    grad_w_router = lax.dot_general(act_two, grad_logits, by_first, preferred_element_type=f32)
    grad_act_two = jnp.concatenate(grad_acts, axis=0).astype(f32) + lax.dot_general(
        grad_logits, w_router, by_rows, preferred_element_type=f32
    )
    grad_gain_two = jnp.sum(grad_act_two * normed_two, axis=0)
    grad_residual = out_grad.reshape(tokens, width).astype(f32) + norm_back(
        grad_act_two * gain_two, normed_two, scale_two
    )
    grad_branch = grad_residual.astype(bf16).reshape(micros, local, width)

    branch_slice = jnp.concatenate(
        [
            spread(grad_branch[m], "head", ag_order if m % 2 == 0 else other_order).reshape(
                slice_rows, width
            )
            for m in range(micros)
        ],
        axis=0,
    )
    grad_mixed = lax.dot_general(
        branch_slice, w_out_here, by_rows, preferred_element_type=f32
    ).astype(bf16)
    grad_w_out = lax.dot_general(mixed_slice, branch_slice, by_first, preferred_element_type=f32)
    grad_w_out = lax.psum_scatter(
        grad_w_out.astype(bf16), "seq", scatter_dimension=0, tiled=True
    ).astype(f32)
    if paired:
        grads3 = attend_back(queries, keys, values, segments, segments, totals, to_pairs(grad_mixed))
        back = from_pairs(jnp.concatenate(grads3, axis=1))
        back_query, back_key, back_value = back[:, :cols], back[:, cols : 2 * cols], back[:, 2 * cols :]
    else:
        back_query, back_key, back_value = [], [], []
        for m in range(micros):
            trio = [[], [], []]
            for a in range(heads_here):
                part = grad_mixed[m * slice_rows : (m + 1) * slice_rows, a * HD : (a + 1) * HD]
                for kept, grad in zip(trio, attend_back(*jobs[m * heads_here + a], part)):
                    kept.append(grad)
            dq, dk, dv = [jnp.concatenate(kept, axis=1) for kept in trio]
            back_query.append(dq)
            back_key.append(lax.psum_scatter(dk, "seq", scatter_dimension=0, tiled=True))
            back_value.append(lax.psum_scatter(dv, "seq", scatter_dimension=0, tiled=True))
        back_query, back_key, back_value = [
            jnp.concatenate(parts, axis=0) for parts in (back_query, back_key, back_value)
        ]

    grad_query_rot = turn(back_query.astype(f32), -1.0)
    grad_key_rot = turn(back_key.astype(f32), -1.0)
    grad_gain_query = jnp.sum(grad_query_rot * query_normed, axis=0)
    grad_gain_key = jnp.sum(grad_key_rot * key_normed, axis=0)
    pull_query = grad_query_rot * gain_query
    pull_key = grad_key_rot * gain_key
    means = jnp.stack(
        [jnp.sum(pull_query * query_normed, axis=1), jnp.sum(pull_key * key_normed, axis=1)]
    )
    means = over_heads(means)
    grad_query_pre = (query_scale * (pull_query - query_normed * means[0][:, None])).astype(bf16)
    grad_key_pre = (key_scale * (pull_key - key_normed * means[1][:, None])).astype(bf16)
    grad_qkv = jnp.concatenate([grad_query_pre, grad_key_pre, back_value], axis=1)
    grad_act = to_owner(
        lax.dot_general(grad_qkv, w_qkv, by_rows, preferred_element_type=f32).astype(bf16)
    )
    grad_w_qkv = lax.dot_general(act_slice, grad_qkv, by_first, preferred_element_type=f32)
    grad_w_qkv = lax.psum_scatter(
        grad_w_qkv.astype(bf16).reshape(heads_of, seqs, weight_rows, 3 * cols),
        "seq",
        scatter_dimension=1,
        tiled=True,
    ).reshape(heads_of, weight_rows, 3 * cols)
    grad_w_qkv = lax.all_to_all(grad_w_qkv, "head", split_axis=0, concat_axis=0, tiled=True)
    grad_w_qkv = grad_w_qkv.reshape(heads_of, weight_rows, 3, cols).transpose(2, 1, 0, 3)
    grad_w_qkv = grad_w_qkv.reshape(3, weight_rows, width).astype(f32)

    grad_gain_one = jnp.sum(grad_act * normed_one, axis=0)
    hidden_grad = grad_residual + norm_back(grad_act * gain_one, normed_one, scale_one)
    hidden_grad = hidden_grad.astype(bf16).reshape(micros, local, width)

    columns = jnp.concatenate([grad_w_router, grad_gain_two[:, None], grad_gain_one[:, None]], axis=1)
    columns = lax.psum_scatter(columns, "head", scatter_dimension=0, tiled=True)
    columns = jnp.concatenate([columns, grad_gain_query[:, None], grad_gain_key[:, None]], axis=1)
    columns = lax.psum_scatter(columns, "seq", scatter_dimension=0, tiled=True)
    return (
        hidden_out,
        hidden_grad,
        columns[:, expert_count + 1],
        grad_w_qkv[0],
        grad_w_qkv[1],
        grad_w_qkv[2],
        columns[:, expert_count + 2],
        columns[:, expert_count + 3],
        grad_w_out,
        columns[:, expert_count],
        columns[:, :expert_count],
        grad_w_gate,
        grad_w_up,
        grad_w_down,
    )


def solution(mesh):
    rows = P(("head", "seq"), None)
    blocks = P(None, ("head", "seq"), None)
    units = P("seq", "head", None)
    vector = P(("head", "seq"))
    in_specs = (
        blocks,
        P(),
        blocks,
        blocks,
        P(),
        rows,
        rows,
        rows,
        P(),
        P(),
        rows,
        P(),
        P(),
        units,
        units,
        units,
    )
    out_specs = (
        blocks,
        blocks,
        vector,
        rows,
        rows,
        rows,
        vector,
        vector,
        rows,
        vector,
        rows,
        units,
        units,
        units,
    )
    return jax.shard_map(body, mesh=mesh, in_specs=in_specs, out_specs=out_specs, check_vma=False)
```
